1024 devices in a mesh: section: 32 (over x, y, core), tensor: 8 (over z_lo), dp: 4 (over z_hi).
Axes of the slice: x: 4, y: 4, z: 32 (z_hi: 4, z_lo: 8; z = z_hi * 8 + z_lo), core: 2. Of those that a mesh axis runs over, the one named last changes fastest.
Arguments:
- fwd_input: bfloat16 [4, 32, 128, 8192], P('dp', 'section', None, 'tensor'), may hold values from -6 to 6
- fwd_positions: int32 [4, 32, 128], P('dp', 'section'), may hold values from 0 to 4095
- key_weight: bfloat16 [32, 8192, 4, 128], P('section', 'tensor'), may hold values from -0.0625 to 0.0625
- stash: bfloat16 [4, 32, 128, 8192], P('dp', 'section', None, 'tensor'), may hold values from -0.26367188 to 0.26367188
- partner: int32 [32], replicated, may hold values from 0 to 31, as said below
- key_grad: bfloat16 [4, 32, 128, 4, 128], P('dp', 'section'), may hold values from -6 to 6
- bwd_positions: int32 [4, 32, 128], P('dp', 'section'), may hold values from 0 to 4095
Outputs:
- key_out: bfloat16 [4, 32, 128, 4, 128], P('dp', 'section', 'tensor')
- grad_in: bfloat16 [4, 32, 128, 8192], P('dp', 'section', None, 'tensor')
- evicted: bfloat16 [4, 32, 128, 8192], P('dp', 'section', None, 'tensor')
- weight_grad: bfloat16 [32, 8192, 4, 128], P('section', ('tensor', 'dp'))
The draws below stay inside these ranges and needn't reach their ends.
Inputs may be any that keep to these rules, and one draw needn't show every extreme that they name: partner[s] = s xor k for one k with 16 <= k < 32, the same k for all sections; it pairs every section of the first half with one of the second half.
All inputs are finite; a program needn't handle non-finite values.
Results may differ from the reference program's by a relative error of at most 0.015.
Values may be sent and summed in bfloat16 or wider, within the bound.
A program may use at most 32 MiB of HBM per device.

```python
import jax
import jax.numpy as jnp
from jax import lax

D = 8192
KVH = 4
HD = 128
ROWS = 128
SEQ = 4096
N_SECTION = 32
N_DP = 4


def draw_partner(key, part):
    mask_value = jax.random.randint(key, (), N_SECTION // 2, N_SECTION, dtype=jnp.int32)
    return jnp.bitwise_xor(jnp.arange(N_SECTION, dtype=jnp.int32), mask_value)


def set_ends(entries, own_key, smallest, top_value):
    longest = entries.shape.index(max(entries.shape))
    spots = []
    for shift in (0, 1):
        where = [jax.random.randint(jax.random.fold_in(own_key, axis), (), 0, length) for axis, length in enumerate(entries.shape)]
        where[longest] = (where[longest] + shift) % entries.shape[longest]
        spots.append(tuple(where))
    return entries.at[spots[0]].set(smallest).at[spots[1]].set(top_value)


def block_scale(rng, dims, pieces, least, high):
    factor_of, own = 1.0, jax.random.fold_in(rng, 6)
    for dim, blocks in pieces:
        steps = jnp.exp(jax.random.uniform(jax.random.fold_in(own, dim), (blocks,), jnp.float32, least / len(pieces), high / len(pieces)))
        factor_of = factor_of * jnp.repeat(steps, dims[dim] // blocks).reshape([-1 if axis == dim else 1 for axis in range(len(dims))])
    return factor_of


def gaussian(stream_key, extent, spread, reach, cuts=(), kind=jnp.bfloat16):
    result = jax.random.normal(stream_key, extent, jnp.float32) * spread
    if len(cuts) > 0:
        result = block_scale(stream_key, extent, cuts, -0.22, 0.18) * result
    return jnp.clip(result, min=-reach, max=reach).astype(kind)


def setup_inputs(seed: int = 0) -> dict:
    key_list = jax.random.split(jax.random.key(seed), 8)
    fwd_input = gaussian(key_list[0], (N_DP, N_SECTION, ROWS, D), 1.0, 6.0, ((0, 4), (1, 32), (3, 8)))
    fwd_positions = set_ends(jax.random.randint(key_list[1], (N_DP, N_SECTION, ROWS), 0, SEQ), jax.random.fold_in(key_list[1], 1), 0, SEQ - 1).astype(jnp.int32)
    key_weight = gaussian(key_list[2], (N_SECTION, D, KVH, HD), D ** -0.5, 0.0625, ((0, 32), (1, 8)))
    stash = gaussian(key_list[3], (N_DP, N_SECTION, ROWS, D), ((ROWS * N_DP) ** -0.5), 0.26367188, ((0, 4), (1, 32), (3, 8)))
    partner = draw_partner(jax.random.fold_in(key_list[7], 71), 0)
    key_grad = gaussian(key_list[5], (N_DP, N_SECTION, ROWS, KVH, HD), 1.0, 6.0, ((0, 4), (1, 32)))
    bwd_positions = set_ends(jax.random.randint(key_list[6], (N_DP, N_SECTION, ROWS), 0, SEQ), jax.random.fold_in(key_list[6], 1), 0, SEQ - 1).astype(jnp.int32)
    return dict(fwd_input=fwd_input, fwd_positions=fwd_positions, key_weight=key_weight, stash=stash, partner=partner, key_grad=key_grad, bwd_positions=bwd_positions)


THETA = 500000.0


def rope_tables(positions, head_size):
    half = head_size // 2
    freqs = THETA ** (-(2.0 * jnp.arange(half, dtype=jnp.float32)) / head_size)
    angles = positions.astype(jnp.float32)[..., None] * freqs
    return jnp.cos(angles), jnp.sin(angles)


def rotate(keys, cosine, sine, sign):
    half = keys.shape[-1] // 2
    first = keys[..., :half]
    second = keys[..., half:]
    return jnp.concatenate([first * cosine - sign * second * sine, second * cosine + sign * first * sine], axis=-1)


def section_work(section, fwd_input, fwd_positions, key_weight, stash, partner, key_grad, bwd_positions):
    inputs = fwd_input[:, section].astype(jnp.float32)
    weight = key_weight[section].astype(jnp.float32)
    proj = jnp.einsum('prd,dhe->prhe', inputs, weight)
    cosine, sine = rope_tables(fwd_positions[:, section], HD)
    key_block = rotate(proj, cosine[:, :, None], sine[:, :, None], 1.0).astype(jnp.bfloat16)
    grads = key_grad[:, section].astype(jnp.float32)
    back_cos, back_sin = rope_tables(bwd_positions[:, section], HD)
    grad_pre = rotate(grads, back_cos[:, :, None], back_sin[:, :, None], -1.0).astype(jnp.bfloat16)
    grad_wide = grad_pre.astype(jnp.float32)
    input_grad = jnp.einsum('prhe,dhe->prd', grad_wide, weight).astype(jnp.bfloat16)
    held = stash[:, partner[section]].astype(jnp.float32)
    parts = jnp.einsum('prd,prhe->pdhe', held, grad_wide).astype(jnp.bfloat16)
    parts = lax.optimization_barrier(parts).astype(jnp.float32)
    weight_grad = jnp.sum(parts, axis=0).astype(jnp.bfloat16)
    return key_block, input_grad, weight_grad


def reference(fwd_input, fwd_positions, key_weight, stash, partner, key_grad, bwd_positions):
    def one_section(section):
        return section_work(section, fwd_input, fwd_positions, key_weight, stash, partner, key_grad, bwd_positions)

    key_all, input_all, weight_grad = lax.map(one_section, jnp.arange(N_SECTION, dtype=jnp.int32))
    key_out = jnp.moveaxis(key_all, 0, 1)
    grad_in = jnp.roll(jnp.moveaxis(input_all, 0, 1), -1, axis=1)
    evicted = jnp.take(fwd_input, partner, axis=1)
    return key_out, grad_in, evicted, weight_grad
```

```python
import functools

import jax
import jax.numpy as jnp
from jax import lax
from jax.experimental import pallas as pl
from jax.experimental.pallas import tpu as pltpu
from jax.sharding import PartitionSpec as P

THETA = 500000.0
MESH = pl.DeviceIdType.MESH
QUAD = 4


def rope_tables(positions, head_size):
    half = head_size // 2
    freqs = THETA ** (-(2.0 * jnp.arange(half, dtype=jnp.float32)) / head_size)
    angles = positions.astype(jnp.float32)[..., None] * freqs
    return (jnp.cos(angles), jnp.sin(angles))


def rotate(keys, cosine, sine, sign):
    half = keys.shape[-1] // 2
    first = keys[..., :half]
    second = keys[..., half:]
    return jnp.concatenate(
        [first * cosine - sign * second * sine, second * cosine + sign * first * sine], axis=-1
    )


def exchange_kernel(
    mask, sizes, fwd, stash, grad, partial, g,
    evicted, grad_in, held, g_all, keys,
    s_send, s_recv, h_send, h_recv, k_send, k_recv, c_send, c_recv, a_send, g_recv, far_ready,
):
    n_s, n_t, n_p = sizes
    n_z = n_t * n_p
    s = lax.axis_index("section")
    t = lax.axis_index("tensor")
    p = lax.axis_index("dp")
    z = p * n_t + t
    partner = s
    for bit in range(n_s.bit_length() - 1):
        if mask >> bit & 1:
            partner = partner + (1 << bit) * (1 - 2 * ((s // (1 << bit)) % 2))
    before = (s + n_s - 1) % n_s
    after = (s + 1) % n_s

    def dp(step):
        return (p + step + n_p) % n_p

    def along(step):
        there = (z + step + n_z) % n_z
        return (s, there % n_t, there // n_t)

    def device(a):
        return {"section": a[0], "tensor": a[1], "dp": a[2]}

    def remote(src, dst, send, recv, a):
        return pltpu.make_async_remote_copy(
            src_ref=src, dst_ref=dst, send_sem=send, recv_sem=recv,
            device_id=device(a), device_id_type=MESH,
        )

    half = (t // QUAD) % 2
    way = 1 - 2 * half
    r = t % QUAD

    peers = [(partner, t, p), (partner, t, dp(1)), (partner, t, dp(-1))]
    peers += [(s, t, dp(1)), (s, t, dp(-1)), along(QUAD), along(-QUAD)]
    peers += [(s, (t + j) % n_t, p) for j in range(1, n_t)]
    barrier = pltpu.get_barrier_semaphore()
    for a in peers + [(before, t, p), (after, t, p)]:
        pl.semaphore_signal(barrier, inc=1, device_id=device(a), device_id_type=MESH)
    pl.semaphore_wait(barrier, len(peers) + 2)

    pl.semaphore_signal(far_ready, inc=1, device_id=device((s, t, dp(-1))), device_id_type=MESH)

    rows = g.shape[0] // QUAD
    mine = pl.ds(pl.multiple_of(r * rows, rows), rows)
    q_near = (p - way + n_p) % n_p
    q_far = (p + way + n_p) % n_p
    q_last = (p + n_p // 2) % n_p

    def step(q, src, slot, to):
        return remote(src, g_all.at[q, mine], c_send.at[slot], g_recv.at[q, r], along(to * QUAD))

    def spread(q, slot):
        copies = []
        for j in range(1, QUAD):
            there = half * QUAD + (r + j) % QUAD
            copies.append(
                remote(
                    g_all.at[q, mine], g_all.at[q, mine], a_send.at[slot, j], g_recv.at[q, r],
                    (s, there, p),
                )
            )
            copies[-1].start()
        return copies

    def arrived(q, block):
        part = g_all.at[q, pl.ds(pl.multiple_of(block * rows, rows), rows)]
        remote(part, part, c_send.at[0], g_recv.at[q, block], (s, t, p)).wait_recv()

    sent = [step(p, g.at[mine], 0, -way)]
    sent[0].start()

    def key_copy(j):
        there = (t + j) % n_t
        block = partial.shape[0] // n_t
        return remote(
            partial.at[pl.ds(pl.multiple_of(there * block, block), block)], keys.at[t],
            k_send.at[j], k_recv.at[t], (s, there, p),
        )

    def held_copy(j):
        there = dp(j)
        width = stash.shape[1] // n_p
        return remote(
            stash.at[:, pl.ds(pl.multiple_of(there * width, width), width)], held.at[p],
            h_send.at[j], h_recv.at[p], (partner, t, there),
        )

    def go(copy):
        copy.start()
        sent.append(copy)

    for j in range(1, n_t):
        go(key_copy(j))
    go(held_copy(1))
    go(held_copy(3))
    go(held_copy(0))
    go(remote(fwd, evicted, s_send.at[0], s_recv.at[0], (partner, t, p)))
    go(remote(grad, grad_in, s_send.at[1], s_recv.at[1], (before, t, p)))

    arrived(q_near, r)
    go(step(q_near, g_all.at[q_near, mine], 1, way))
    sent += spread(q_near, 0)
    arrived(q_far, r)
    go(step(q_far, g_all.at[q_far, mine], 2, -way))
    sent += spread(q_far, 1)
    pl.semaphore_wait(far_ready, 1)
    go(held_copy(2))
    arrived(q_last, r)
    sent += spread(q_last, 2)

    for q in (q_near, q_far, q_last):
        for j in range(1, QUAD):
            arrived(q, (r + j) % QUAD)
    for j in range(1, n_t):
        block = keys.at[(t + j) % n_t]
        remote(block, block, k_send.at[j], k_recv.at[(t + j) % n_t], (s, t, p)).wait_recv()
    for j in range(n_p):
        block = held.at[dp(j)]
        remote(block, block, h_send.at[j], h_recv.at[dp(j)], (s, t, p)).wait_recv()
    remote(fwd, evicted, s_send.at[0], s_recv.at[0], (partner, t, p)).wait_recv()
    remote(grad, grad_in, s_send.at[1], s_recv.at[1], (before, t, p)).wait_recv()
    for copy in sent:
        copy.wait_send()


def exchange(mask, sizes, fwd, stash, grad, partial, g):
    n_s, n_t, n_p = sizes
    dtype = fwd.dtype
    tokens, width = fwd.shape
    columns = g.shape[1]
    dma = pltpu.SemaphoreType.DMA
    anywhere = pl.BlockSpec(memory_space=pl.ANY)
    shapes = [
        (tokens, width), (tokens, width), (n_p, tokens, width // n_p), (n_p, tokens, columns),
        (n_t, tokens // n_t, columns),
    ]
    return pl.pallas_call(
        functools.partial(exchange_kernel, mask, sizes),
        out_shape=[jax.ShapeDtypeStruct(shape, dtype) for shape in shapes],
        in_specs=[anywhere] * 5,
        out_specs=[anywhere] * 5,
        scratch_shapes=[
            dma((2,)), dma((2,)), dma((n_p,)), dma((n_p,)), dma((n_t,)), dma((n_t,)),
            dma((3,)), dma((n_p, QUAD)), dma((3, QUAD)), dma((n_p, QUAD)),
            pltpu.SemaphoreType.REGULAR,
        ],
        compiler_params=pltpu.CompilerParams(collective_id=mask % (n_s // 2), has_side_effects=True),
        name=f"exchange_{mask}",
    )(fwd, stash, grad, partial, g)


def body(sizes, fwd_input, fwd_positions, key_weight, stash, partner, key_grad, bwd_positions):
    n_s, n_t, n_p = sizes
    inputs = fwd_input[0, 0]
    weight = key_weight[0]
    width_local, head_count, head_size = weight.shape
    columns = head_count * head_size
    flat_weight = weight.reshape(width_local, columns)
    tokens = inputs.shape[0]
    my_rows = tokens // n_t
    partial = jnp.dot(inputs, flat_weight, preferred_element_type=jnp.float32).astype(jnp.bfloat16)
    grads = key_grad[0, 0].astype(jnp.float32)
    back_cos, back_sin = rope_tables(bwd_positions[0, 0], head_size)
    grad_pre = rotate(grads, back_cos[:, None], back_sin[:, None], -1.0).astype(jnp.bfloat16)
    g = grad_pre.reshape(tokens, columns)
    input_grad = jnp.einsum("rn,dn->rd", g, flat_weight, preferred_element_type=jnp.float32)
    input_grad = input_grad.astype(jnp.bfloat16)

    first_mask = n_s // 2
    branches = [
        functools.partial(exchange, mask, sizes) for mask in range(first_mask, 2 * first_mask)
    ]
    evicted, grad_in, held, g_all, keys = lax.switch(
        partner[0] - first_mask, branches, inputs, stash[0, 0], input_grad, partial, g
    )

    me_t = lax.axis_index("tensor")
    me_p = lax.axis_index("dp")
    row_start = me_t * my_rows
    own = lax.dynamic_slice_in_dim(partial, row_start, my_rows, 0)
    is_own = (jnp.arange(n_t, dtype=jnp.int32) == me_t)[:, None, None]
    summed = jnp.sum(jnp.where(is_own, own[None], keys).astype(jnp.float32), axis=0)
    summed = summed.reshape(my_rows, head_count, head_size)
    my_positions = lax.dynamic_slice_in_dim(fwd_positions[0, 0], row_start, my_rows, 0)
    cosine, sine = rope_tables(my_positions, head_size)
    key_out = rotate(summed, cosine[:, None], sine[:, None], 1.0).astype(jnp.bfloat16)

    g_all = lax.dynamic_update_slice_in_dim(g_all, g[None], me_p, 0)
    weight_grad = jnp.einsum("prd,prn->dn", held, g_all, preferred_element_type=jnp.float32)
    weight_grad = weight_grad.astype(jnp.bfloat16).reshape(-1, head_count, head_size)
    return key_out[None, None], grad_in[None, None], evicted[None, None], weight_grad[None]


def solution(mesh):
    sizes = (mesh.shape["section"], mesh.shape["tensor"], mesh.shape["dp"])
    placed = (
        P("dp", "section", None, "tensor"),
        P("dp", "section", None),
        P("section", "tensor", None, None),
        P("dp", "section", None, "tensor"),
        P(),
        P("dp", "section", None, None, None),
        P("dp", "section", None),
    )
    return jax.shard_map(
        functools.partial(body, sizes),
        mesh=mesh,
        in_specs=placed,
        out_specs=(
            P("dp", "section", "tensor", None, None),
            P("dp", "section", None, "tensor"),
            P("dp", "section", None, "tensor"),
            P("section", ("tensor", "dp"), None, None),
        ),
        check_vma=False,
    )
```

```python
import functools

import jax
import jax.numpy as jnp
from jax import lax
from jax.experimental import pallas as pl
from jax.experimental.pallas import tpu as pltpu
from jax.sharding import PartitionSpec as P

THETA = 500000.0
MESH = pl.DeviceIdType.MESH
QUAD = 4


def rope_tables(positions, head_size):
    half = head_size // 2
    freqs = THETA ** (-(2.0 * jnp.arange(half, dtype=jnp.float32)) / head_size)
    angles = positions.astype(jnp.float32)[..., None] * freqs
    return (jnp.cos(angles), jnp.sin(angles))


def rotate(keys, cosine, sine, sign):
    half = keys.shape[-1] // 2
    first = keys[..., :half]
    second = keys[..., half:]
    return jnp.concatenate(
        [first * cosine - sign * second * sine, second * cosine + sign * first * sine], axis=-1
    )


def exchange_kernel(
    mask, sizes, fwd, stash, grad, partial, g,
    evicted, grad_in, held, g_all, keys,
    k_parts, k_sum,
    s_send, s_recv, h_send, h_recv, k_send, k_recv, c_send, c_recv, own_sem, own_g_sem, near_ready, pair_ready,
    far_ready, last_ready,
):
    n_s, n_t, n_p = sizes
    n_z = n_t * n_p
    s = lax.axis_index("section")
    t = lax.axis_index("tensor")
    p = lax.axis_index("dp")
    z = p * n_t + t
    partner = s
    for bit in range(n_s.bit_length() - 1):
        if mask >> bit & 1:
            partner = partner + (1 << bit) * (1 - 2 * ((s // (1 << bit)) % 2))
    before = (s + n_s - 1) % n_s
    after = (s + 1) % n_s
    half = (t // QUAD) % 2
    way = 1 - 2 * half
    r = t % QUAD

    def dp(step):
        return (p + step + n_p) % n_p

    def along(step):
        there = (z + step + n_z) % n_z
        return (s, there % n_t, there // n_t)

    def mate(j):
        return (s, half * QUAD + (r + j) % QUAD, p)

    def device(a):
        return {"section": a[0], "tensor": a[1], "dp": a[2]}

    def signal(sem, a):
        pl.semaphore_signal(sem, inc=1, device_id=device(a), device_id_type=MESH)

    def remote(src, dst, send, recv, a):
        return pltpu.make_async_remote_copy(
            src_ref=src, dst_ref=dst, send_sem=send, recv_sem=recv,
            device_id=device(a), device_id_type=MESH,
        )

    peers = [(partner, t, p), (before, t, p), (after, t, p)]
    peers += [along(j) for j in (-QUAD, QUAD, -2, 2, -1, 1)]
    peers += [mate(j) for j in range(1, QUAD)]
    barrier = pltpu.get_barrier_semaphore()
    for a in peers:
        signal(barrier, a)
    block = k_sum.shape[1]
    own_part = pltpu.make_async_copy(partial.at[:, r], k_parts.at[0], own_sem)
    own_part.start()
    own_g = pltpu.make_async_copy(g, g_all.at[p], own_g_sem)
    own_g.start()
    pl.semaphore_wait(barrier, len(peers))

    sent = []

    def go(copy, when=None):
        if when is None:
            copy.start()
        else:
            pl.when(when)(copy.start)
        sent.append((copy, when))

    signal(near_ready, along(QUAD))
    signal(near_ready, along(-QUAD))

    rows = g.shape[0] // QUAD
    base = pl.multiple_of(r * rows, rows)
    q_near = (p - way + n_p) % n_p
    q_far = (p + way + n_p) % n_p
    q_last = (p + n_p // 2) % n_p

    def piece(src, q, slot, there, start, size, i):
        at = pl.ds(start, size)
        return remote(src.at[at], g_all.at[q, at], c_send.at[slot, i], c_recv.at[q, i], there)

    def step(src, q, slot, to):
        return piece(src, q, slot, along(to * QUAD), base, rows, 0)

    def spread(src, q, slot):
        small = rows // 2
        plans = ((1, 0, rows, 1), (-1, 0, rows, 2), (2, 0, small, 3), (-2, small, small, 4))
        for to, offset, size, i in plans:
            there = along(to)
            start = pl.multiple_of(base + offset, small)
            go(piece(src, q, slot, there, start, size, i), there[2] != q)

    def arrived(q, i):
        small = rows // 2
        back, offset, size = ((0, 0, rows), (1, 0, rows), (-1, 0, rows), (2, 0, small), (-2, small, small))[i]
        start = pl.multiple_of(((r - back + QUAD) % QUAD) * rows + offset, small)
        piece(g_all.at[q], q, 0, (s, t, p), start, size, i).wait_recv()

    go(step(g, p, 0, -way))
    spread(g, p, 0)
    for j in range(1, QUAD):
        go(remote(partial.at[:, (r + j) % QUAD], k_parts.at[QUAD - j], k_send.at[j], k_recv.at[QUAD - j], mate(j)))

    def held_copy(j):
        there = dp(j)
        width = stash.shape[1] // n_p
        return remote(
            stash.at[:, pl.ds(pl.multiple_of(there * width, width), width)], held.at[p],
            h_send.at[j], h_recv.at[p], (partner, t, there),
        )

    pl.semaphore_wait(near_ready, 2)
    signal(pair_ready, (partner, t, p))
    signal(far_ready, (s, t, dp(-1)))

    arrived(q_near, 0)
    go(step(g_all.at[q_near], q_near, 1, way))
    spread(g_all.at[q_near], q_near, 1)

    pl.semaphore_wait(pair_ready, 1)
    go(held_copy(1))
    go(held_copy(3))
    go(held_copy(0))
    go(remote(fwd, evicted, s_send.at[0], s_recv.at[0], (partner, t, p)))
    go(remote(grad, grad_in, s_send.at[1], s_recv.at[1], (before, t, p)))

    own_part.wait()
    for j in range(1, QUAD):
        remote(k_parts.at[j], k_parts.at[j], k_send.at[j], k_recv.at[j], (s, t, p)).wait_recv()
    total = k_parts[0].astype(jnp.float32)
    for j in range(1, QUAD):
        total = total + k_parts[j].astype(jnp.float32)
    k_sum[...] = total.astype(k_sum.dtype)

    pl.semaphore_wait(far_ready, 1)
    signal(last_ready, (partner, t, p))
    arrived(q_far, 0)
    go(step(g_all.at[q_far], q_far, 2, -way))
    spread(g_all.at[q_far], q_far, 2)
    own_keys = pltpu.make_async_copy(k_sum.at[half], keys.at[0], own_sem)
    own_keys.start()
    go(remote(k_sum.at[1 - half], keys.at[1], k_send.at[0], k_recv.at[0], along(way * QUAD)))

    pl.semaphore_wait(last_ready, 1)
    go(held_copy(2))
    arrived(q_last, 0)
    spread(g_all.at[q_last], q_last, 3)

    for q in (q_near, q_far, q_last):
        for i in range(1, 5):
            arrived(q, i)
    own_g.wait()
    own_keys.wait()
    remote(k_sum.at[0], keys.at[1], k_send.at[0], k_recv.at[0], (s, t, p)).wait_recv()
    for j in range(n_p):
        part = held.at[dp(j)]
        remote(part, part, h_send.at[j], h_recv.at[dp(j)], (s, t, p)).wait_recv()
    remote(fwd, evicted, s_send.at[0], s_recv.at[0], (partner, t, p)).wait_recv()
    remote(grad, grad_in, s_send.at[1], s_recv.at[1], (before, t, p)).wait_recv()
    for copy, when in sent:
        if when is None:
            copy.wait_send()
        else:
            pl.when(when)(copy.wait_send)


def exchange(mask, sizes, fwd, stash, grad, partial, g):
    n_s, n_t, n_p = sizes
    dtype = fwd.dtype
    tokens, width = fwd.shape
    columns = partial.shape[1]
    block = tokens // n_t
    dma = pltpu.SemaphoreType.DMA
    anywhere = pl.BlockSpec(memory_space=pl.ANY)
    shapes = [
        (tokens, width), (tokens, width), (n_p, tokens, width // n_p), (n_p, *g.shape),
        (2, block, columns),
    ]
    return pl.pallas_call(
        functools.partial(exchange_kernel, mask, sizes),
        out_shape=[jax.ShapeDtypeStruct(shape, dtype) for shape in shapes],
        in_specs=[anywhere] * 5,
        out_specs=[anywhere] * 5,
        scratch_shapes=[
            pltpu.VMEM((QUAD, 2, block, columns), dtype),
            pltpu.VMEM((2, block, columns), dtype),
            dma((2,)), dma((2,)), dma((n_p,)), dma((n_p,)), dma((QUAD,)), dma((QUAD,)),
            dma((4, 5)), dma((n_p, 5)), dma, dma,
        ] + [pltpu.SemaphoreType.REGULAR] * 4,
        compiler_params=pltpu.CompilerParams(collective_id=mask % (n_s // 2), has_side_effects=True),
        name=f"exchange_{mask}",
    )(fwd, stash, grad, partial.reshape(2, QUAD, block, columns), g)


def finish_kernel(
    evicted, grad_in, held, g_all, keys, positions, freqs,
    evicted_out, grad_out, key_out, weight_out, k_buffer, w_buffer, at_buffer, angles, sems,
):
    copies = [
        pltpu.make_async_copy(evicted, evicted_out, sems.at[0]),
        pltpu.make_async_copy(grad_in, grad_out, sems.at[1]),
    ]
    for copy in copies:
        copy.start()
    fetch = pltpu.make_async_copy(positions, at_buffer, sems.at[4])
    fetch.start()
    total = None
    for q in range(held.shape[0]):
        one = lax.dot_general(
            held[q], g_all[q], (((0,), (0,)), ((), ())), preferred_element_type=jnp.float32
        )
        total = one if total is None else total + one
    w_buffer[...] = total.reshape(w_buffer.shape).astype(w_buffer.dtype)
    copies.append(pltpu.make_async_copy(w_buffer, weight_out, sems.at[3]))
    copies[-1].start()

    rows, heads, size = k_buffer.shape
    fetch.wait()
    tokens = at_buffer.shape[1]
    spread = jnp.broadcast_to(at_buffer[...].astype(jnp.float32), (size, tokens))
    angles[...] = spread.T * freqs[...]
    start = pl.multiple_of(lax.axis_index("tensor") * rows, rows)
    mine = angles[pl.ds(start, rows), :]
    upper = lax.broadcasted_iota(jnp.int32, mine.shape, 1) >= size // 2
    cosine, sine = jnp.cos(mine), jnp.sin(mine)
    sine = jnp.where(upper, sine, -sine)
    summed = keys[0].astype(jnp.float32) + keys[1].astype(jnp.float32)
    turned = []
    for h in range(heads):
        x = summed[:, h * size : (h + 1) * size]
        turned.append(x * cosine + pltpu.roll(x, size // 2, 1) * sine)
    turned = jnp.concatenate(turned, axis=1)
    k_buffer[...] = turned.reshape(k_buffer.shape).astype(k_buffer.dtype)
    copies.append(pltpu.make_async_copy(k_buffer, key_out, sems.at[2]))
    copies[-1].start()
    for copy in copies:
        copy.wait()


def finish(heads, size, evicted, grad_in, held, g_all, keys, positions):
    half = size // 2
    freqs = THETA ** (-(2.0 * jnp.arange(half, dtype=jnp.float32)) / size)
    freqs = jnp.concatenate([freqs, freqs])[None]
    anywhere = pl.BlockSpec(memory_space=pl.ANY)
    vmem = pl.BlockSpec(memory_space=pltpu.VMEM)
    dtype = evicted.dtype
    k_shape = (keys.shape[1], heads, size)
    w_shape = (held.shape[2], heads, size)
    shapes = (evicted.shape, grad_in.shape, k_shape, w_shape)
    return pl.pallas_call(
        finish_kernel,
        out_shape=[jax.ShapeDtypeStruct(shape, dtype) for shape in shapes],
        in_specs=[anywhere] * 2 + [vmem] * 3 + [anywhere, vmem],
        out_specs=[anywhere] * 4,
        scratch_shapes=[
            pltpu.VMEM(k_shape, dtype), pltpu.VMEM(w_shape, dtype),
            pltpu.VMEM(positions.shape, jnp.int32), pltpu.VMEM((positions.shape[1], size), jnp.float32),
            pltpu.SemaphoreType.DMA((5,)),
        ],
        name="finish",
    )(evicted, grad_in, held, g_all, keys, positions, freqs)


def body(sizes, fwd_input, fwd_positions, key_weight, stash, partner, key_grad, bwd_positions):
    n_s, n_t, n_p = sizes
    inputs = fwd_input[0, 0]
    weight = key_weight[0]
    width_local, head_count, head_size = weight.shape
    columns = head_count * head_size
    flat_weight = weight.reshape(width_local, columns)
    tokens = inputs.shape[0]
    partial = jnp.dot(inputs, flat_weight, preferred_element_type=jnp.float32).astype(jnp.bfloat16)
    grads = key_grad[0, 0].astype(jnp.float32)
    back_cos, back_sin = rope_tables(bwd_positions[0, 0], head_size)
    g = rotate(grads, back_cos[:, None], back_sin[:, None], -1.0).astype(jnp.bfloat16)
    flat_g = g.reshape(tokens, columns)
    input_grad = jnp.einsum("rn,dn->rd", flat_g, flat_weight, preferred_element_type=jnp.float32)
    input_grad = input_grad.astype(jnp.bfloat16)

    flat_g = lax.optimization_barrier(flat_g)

    first_mask = n_s // 2
    branches = [
        functools.partial(exchange, mask, sizes) for mask in range(first_mask, 2 * first_mask)
    ]
    evicted, grad_in, held, g_all, keys = lax.switch(
        partner[0] - first_mask, branches, inputs, stash[0, 0], input_grad, partial, flat_g
    )

    evicted, grad_in, key_out, weight_grad = finish(
        head_count, head_size, evicted, grad_in, held, g_all, keys, fwd_positions[0]
    )
    return key_out[None, None], grad_in[None, None], evicted[None, None], weight_grad[None]


def solution(mesh):
    sizes = (mesh.shape["section"], mesh.shape["tensor"], mesh.shape["dp"])
    placed = (
        P("dp", "section", None, "tensor"),
        P("dp", "section", None),
        P("section", "tensor", None, None),
        P("dp", "section", None, "tensor"),
        P(),
        P("dp", "section", None, None, None),
        P("dp", "section", None),
    )
    return jax.shard_map(
        functools.partial(body, sizes),
        mesh=mesh,
        in_specs=placed,
        out_specs=(
            P("dp", "section", "tensor", None, None),
            P("dp", "section", None, "tensor"),
            P("dp", "section", None, "tensor"),
            P("section", ("tensor", "dp"), None, None),
        ),
        check_vma=False,
    )
```

```python
import functools

import jax
import jax.numpy as jnp
from jax import lax
from jax.experimental import pallas as pl
from jax.experimental.pallas import tpu as pltpu
from jax.sharding import PartitionSpec as P

THETA = 500000.0
MESH = pl.DeviceIdType.MESH
QUAD = 4


def rope_tables(positions, head_size):
    half = head_size // 2
    freqs = THETA ** (-(2.0 * jnp.arange(half, dtype=jnp.float32)) / head_size)
    angles = positions.astype(jnp.float32)[..., None] * freqs
    return (jnp.cos(angles), jnp.sin(angles))


def rotate(keys, cosine, sine, sign):
    half = keys.shape[-1] // 2
    first = keys[..., :half]
    second = keys[..., half:]
    return jnp.concatenate(
        [first * cosine - sign * second * sine, second * cosine + sign * first * sine], axis=-1
    )


def exchange_kernel(
    mask, sizes, fwd, stash, grad, partial, g,
    evicted, grad_in, held, g_all, keys,
    k_parts, k_sum,
    s_send, s_recv, h_send, h_recv, k_send, k_recv, c_send, c_recv, own_sem, own_g_sem, near_ready, pair_ready,
    far_ready, last_ready,
):
    n_s, n_t, n_p = sizes
    n_z = n_t * n_p
    s = lax.axis_index("section")
    t = lax.axis_index("tensor")
    p = lax.axis_index("dp")
    z = p * n_t + t
    partner = s
    for bit in range(n_s.bit_length() - 1):
        if mask >> bit & 1:
            partner = partner + (1 << bit) * (1 - 2 * ((s // (1 << bit)) % 2))
    before = (s + n_s - 1) % n_s
    after = (s + 1) % n_s
    half = (t // QUAD) % 2
    way = 1 - 2 * half
    r = t % QUAD

    def dp(step):
        return (p + step + n_p) % n_p

    def along(step):
        there = (z + step + n_z) % n_z
        return (s, there % n_t, there // n_t)

    def mate(j):
        return (s, half * QUAD + (r + j) % QUAD, p)

    def device(a):
        return {"section": a[0], "tensor": a[1], "dp": a[2]}

    def signal(sem, a):
        pl.semaphore_signal(sem, inc=1, device_id=device(a), device_id_type=MESH)

    def remote(src, dst, send, recv, a):
        return pltpu.make_async_remote_copy(
            src_ref=src, dst_ref=dst, send_sem=send, recv_sem=recv,
            device_id=device(a), device_id_type=MESH,
        )

    peers = [(partner, t, p), (before, t, p), (after, t, p)]
    peers += [along(j) for j in (-QUAD, QUAD, -2, 2, -1, 1)]
    peers += [mate(j) for j in range(1, QUAD)]
    barrier = pltpu.get_barrier_semaphore()
    for a in peers:
        signal(barrier, a)
    block = k_sum.shape[1]
    own_part = pltpu.make_async_copy(partial.at[:, r], k_parts.at[0], own_sem)
    own_part.start()
    own_g = pltpu.make_async_copy(g, g_all.at[p], own_g_sem)
    own_g.start()
    pl.semaphore_wait(barrier, len(peers))

    sent = []

    def go(copy, when=None):
        if when is None:
            copy.start()
        else:
            pl.when(when)(copy.start)
        sent.append((copy, when))

    signal(near_ready, along(QUAD))
    signal(near_ready, along(-QUAD))

    rows = g.shape[0] // QUAD
    base = pl.multiple_of(r * rows, rows)
    q_near = (p - way + n_p) % n_p
    q_far = (p + way + n_p) % n_p
    q_last = (p + n_p // 2) % n_p

    def piece(src, q, slot, there, start, size, i):
        at = pl.ds(start, size)
        return remote(src.at[at], g_all.at[q, at], c_send.at[slot, i], c_recv.at[q, i], there)

    def step(src, q, slot, to):
        return piece(src, q, slot, along(to * QUAD), base, rows, 0)

    def spread(src, q, slot):
        small = rows // 2
        plans = ((1, 0, rows, 1), (-1, 0, rows, 2), (2, 0, small, 3), (-2, small, small, 4))
        for to, offset, size, i in plans:
            there = along(to)
            start = pl.multiple_of(base + offset, small)
            go(piece(src, q, slot, there, start, size, i), there[2] != q)

    def arrived(q, i):
        small = rows // 2
        back, offset, size = ((0, 0, rows), (1, 0, rows), (-1, 0, rows), (2, 0, small), (-2, small, small))[i]
        start = pl.multiple_of(((r - back + QUAD) % QUAD) * rows + offset, small)
        piece(g_all.at[q], q, 0, (s, t, p), start, size, i).wait_recv()

    go(step(g, p, 0, -way))
    spread(g, p, 0)
    for j in range(1, QUAD):
        go(remote(partial.at[:, (r + j) % QUAD], k_parts.at[QUAD - j], k_send.at[j], k_recv.at[QUAD - j], mate(j)))

    def held_copy(j):
        there = dp(j)
        width = stash.shape[1] // n_p
        return remote(
            stash.at[:, pl.ds(pl.multiple_of(there * width, width), width)], held.at[p],
            h_send.at[j], h_recv.at[p], (partner, t, there),
        )

    pl.semaphore_wait(near_ready, 2)
    signal(pair_ready, (partner, t, p))
    signal(far_ready, (s, t, dp(-1)))

    arrived(q_near, 0)
    go(step(g_all.at[q_near], q_near, 1, way))
    spread(g_all.at[q_near], q_near, 1)

    pl.semaphore_wait(pair_ready, 1)
    go(held_copy(1))
    go(held_copy(3))
    go(held_copy(0))
    go(remote(fwd, evicted, s_send.at[0], s_recv.at[0], (partner, t, p)))
    go(remote(grad, grad_in, s_send.at[1], s_recv.at[1], (before, t, p)))

    own_part.wait()
    for j in range(1, QUAD):
        remote(k_parts.at[j], k_parts.at[j], k_send.at[j], k_recv.at[j], (s, t, p)).wait_recv()
    total = k_parts[0].astype(jnp.float32)
    for j in range(1, QUAD):
        total = total + k_parts[j].astype(jnp.float32)
    k_sum[...] = total.astype(k_sum.dtype)

    pl.semaphore_wait(far_ready, 1)
    signal(last_ready, (partner, t, p))
    arrived(q_far, 0)
    go(step(g_all.at[q_far], q_far, 2, -way))
    spread(g_all.at[q_far], q_far, 2)
    own_keys = pltpu.make_async_copy(k_sum.at[half], keys.at[0], own_sem)
    own_keys.start()
    go(remote(k_sum.at[1 - half], keys.at[1], k_send.at[0], k_recv.at[0], along(way * QUAD)))

    pl.semaphore_wait(last_ready, 1)
    go(held_copy(2))
    arrived(q_last, 0)
    spread(g_all.at[q_last], q_last, 3)

    for q in (q_near, q_far, q_last):
        for i in range(1, 5):
            arrived(q, i)
    own_g.wait()
    own_keys.wait()
    remote(k_sum.at[0], keys.at[1], k_send.at[0], k_recv.at[0], (s, t, p)).wait_recv()
    for j in range(n_p):
        part = held.at[dp(j)]
        remote(part, part, h_send.at[j], h_recv.at[dp(j)], (s, t, p)).wait_recv()
    remote(fwd, evicted, s_send.at[0], s_recv.at[0], (partner, t, p)).wait_recv()
    remote(grad, grad_in, s_send.at[1], s_recv.at[1], (before, t, p)).wait_recv()
    for copy, when in sent:
        if when is None:
            copy.wait_send()
        else:
            pl.when(when)(copy.wait_send)


def exchange(mask, sizes, fwd, stash, grad, partial, g):
    n_s, n_t, n_p = sizes
    dtype = fwd.dtype
    tokens, width = fwd.shape
    columns = partial.shape[1]
    block = tokens // n_t
    dma = pltpu.SemaphoreType.DMA
    anywhere = pl.BlockSpec(memory_space=pl.ANY)
    shapes = [
        (tokens, width), (tokens, width), (n_p, tokens, width // n_p), (n_p, *g.shape),
        (2, block, columns),
    ]
    return pl.pallas_call(
        functools.partial(exchange_kernel, mask, sizes),
        out_shape=[jax.ShapeDtypeStruct(shape, dtype) for shape in shapes],
        in_specs=[anywhere] * 5,
        out_specs=[anywhere] * 5,
        scratch_shapes=[
            pltpu.VMEM((QUAD, 2, block, columns), dtype),
            pltpu.VMEM((2, block, columns), dtype),
            dma((2,)), dma((2,)), dma((n_p,)), dma((n_p,)), dma((QUAD,)), dma((QUAD,)),
            dma((4, 5)), dma((n_p, 5)), dma, dma,
        ] + [pltpu.SemaphoreType.REGULAR] * 4,
        compiler_params=pltpu.CompilerParams(collective_id=mask % (n_s // 2), has_side_effects=True),
        name=f"exchange_{mask}",
    )(fwd, stash, grad, partial.reshape(2, QUAD, block, columns), g)


def finish_kernel(
    evicted, grad_in, held, g_all, keys, positions, freqs,
    evicted_out, grad_out, key_out, weight_out, k_buffer, w_buffer, at_buffer, angles, sems,
):
    copies = [
        pltpu.make_async_copy(evicted, evicted_out, sems.at[0]),
        pltpu.make_async_copy(grad_in, grad_out, sems.at[1]),
    ]
    for copy in copies:
        copy.start()
    fetch = pltpu.make_async_copy(positions, at_buffer, sems.at[4])
    fetch.start()
    total = None
    for q in range(held.shape[0]):
        one = lax.dot_general(
            held[q], g_all[q], (((0,), (0,)), ((), ())), preferred_element_type=jnp.float32
        )
        total = one if total is None else total + one
    w_buffer[...] = total.reshape(w_buffer.shape).astype(w_buffer.dtype)
    copies.append(pltpu.make_async_copy(w_buffer, weight_out, sems.at[3]))
    copies[-1].start()

    rows, heads, size = k_buffer.shape
    fetch.wait()
    tokens = at_buffer.shape[1]
    spread = jnp.broadcast_to(at_buffer[...].astype(jnp.float32), (size, tokens))
    angles[...] = spread.T * freqs[...]
    start = pl.multiple_of(lax.axis_index("tensor") * rows, rows)
    mine = angles[pl.ds(start, rows), :]
    upper = lax.broadcasted_iota(jnp.int32, mine.shape, 1) >= size // 2
    cosine, sine = jnp.cos(mine), jnp.sin(mine)
    sine = jnp.where(upper, sine, -sine)
    summed = keys[0].astype(jnp.float32) + keys[1].astype(jnp.float32)
    turned = []
    for h in range(heads):
        x = summed[:, h * size : (h + 1) * size]
        turned.append(x * cosine + pltpu.roll(x, size // 2, 1) * sine)
    turned = jnp.concatenate(turned, axis=1)
    k_buffer[...] = turned.reshape(k_buffer.shape).astype(k_buffer.dtype)
    copies.append(pltpu.make_async_copy(k_buffer, key_out, sems.at[2]))
    copies[-1].start()
    for copy in copies:
        copy.wait()


def finish(heads, size, evicted, grad_in, held, g_all, keys, positions):
    half = size // 2
    freqs = THETA ** (-(2.0 * jnp.arange(half, dtype=jnp.float32)) / size)
    freqs = jnp.concatenate([freqs, freqs])[None]
    anywhere = pl.BlockSpec(memory_space=pl.ANY)
    vmem = pl.BlockSpec(memory_space=pltpu.VMEM)
    dtype = evicted.dtype
    k_shape = (keys.shape[1], heads, size)
    w_shape = (held.shape[2], heads, size)
    shapes = (evicted.shape, grad_in.shape, k_shape, w_shape)
    return pl.pallas_call(
        finish_kernel,
        out_shape=[jax.ShapeDtypeStruct(shape, dtype) for shape in shapes],
        in_specs=[anywhere] * 2 + [vmem] * 3 + [anywhere, vmem],
        out_specs=[anywhere] * 4,
        scratch_shapes=[
            pltpu.VMEM(k_shape, dtype), pltpu.VMEM(w_shape, dtype),
            pltpu.VMEM(positions.shape, jnp.int32), pltpu.VMEM((positions.shape[1], size), jnp.float32),
            pltpu.SemaphoreType.DMA((5,)),
        ],
        name="finish",
    )(evicted, grad_in, held, g_all, keys, positions, freqs)


def body(sizes, fwd_input, fwd_positions, key_weight, stash, partner, key_grad, bwd_positions):
    n_s, n_t, n_p = sizes
    inputs = fwd_input[0, 0]
    weight = key_weight[0]
    width_local, head_count, head_size = weight.shape
    columns = head_count * head_size
    flat_weight = weight.reshape(width_local, columns)
    tokens = inputs.shape[0]
    grads = key_grad[0, 0].astype(jnp.float32)
    back_cos, back_sin = rope_tables(bwd_positions[0, 0], head_size)
    g = rotate(grads, back_cos[:, None], back_sin[:, None], -1.0).astype(jnp.bfloat16)
    flat_g = g.reshape(tokens, columns)
    input_grad = jnp.einsum("rn,dn->rd", flat_g, flat_weight, preferred_element_type=jnp.float32)
    input_grad = input_grad.astype(jnp.bfloat16)

    flat_g, inputs = lax.optimization_barrier((flat_g, inputs))
    partial = jnp.dot(inputs, flat_weight, preferred_element_type=jnp.float32).astype(jnp.bfloat16)

    first_mask = n_s // 2
    branches = [
        functools.partial(exchange, mask, sizes) for mask in range(first_mask, 2 * first_mask)
    ]
    evicted, grad_in, held, g_all, keys = lax.switch(
        partner[0] - first_mask, branches, inputs, stash[0, 0], input_grad, partial, flat_g
    )

    evicted, grad_in, key_out, weight_grad = finish(
        head_count, head_size, evicted, grad_in, held, g_all, keys, fwd_positions[0]
    )
    return key_out[None, None], grad_in[None, None], evicted[None, None], weight_grad[None]


def solution(mesh):
    sizes = (mesh.shape["section"], mesh.shape["tensor"], mesh.shape["dp"])
    placed = (
        P("dp", "section", None, "tensor"),
        P("dp", "section", None),
        P("section", "tensor", None, None),
        P("dp", "section", None, "tensor"),
        P(),
        P("dp", "section", None, None, None),
        P("dp", "section", None),
    )
    return jax.shard_map(
        functools.partial(body, sizes),
        mesh=mesh,
        in_specs=placed,
        out_specs=(
            P("dp", "section", "tensor", None, None),
            P("dp", "section", None, "tensor"),
            P("dp", "section", None, "tensor"),
            P("section", ("tensor", "dp"), None, None),
        ),
        check_vma=False,
    )
```
